256 devices in a mesh: tm: 32 (over y_lo, z, core), gy: 8 (over y_hi, x).
Axes of the slice: x: 4, y: 4 (y_hi: 2, y_lo: 2; y = y_hi * 2 + y_lo), z: 8, core: 2. Of those that a mesh axis runs over, the one named last changes fastest.
Arguments:
- magnetic: bfloat16 [32, 3, 3, 1024, 1024], P('tm', None, None, 'gy'), may hold values from -6 to 6
- velocity: bfloat16 [32, 3, 1, 1024, 1024], P('tm', None, None, 'gy'), may hold values from -6 to 6
- mode_bin: int32 [1024, 1024], P(None, 'gy'), may hold values from 0 to 127, as said below
- omega_edges: int32 [9], replicated, may hold values from 0 to 32, as said below
Outputs:
- power: float32 [32, 1024, 1024], P('tm', None, 'gy')
- spectrum: float32 [8, 128], replicated
The draws below stay inside these ranges and needn't reach their ends.
Inputs may be any that keep to these rules, and one draw needn't show every extreme that they name: mode_bin = 16 * p + q, where p is a level of min(kz, 1024 - kz) and q a level of min(ky, 1024 - ky); levels never fall as the wavenumber rises, and every value occurs. `omega_edges`: edges rise strictly, the first 0 and the last 32.
All inputs are finite; a program needn't handle non-finite values.
Results may differ from the reference program's by a relative error of at most 0.004.
The reference program's roundings to bfloat16 on the way count: a program that leaves them out, or rounds other values in their place, can miss the bound.
Values may be sent and summed in bfloat16 or wider, within the bound.
No kernel may reach another device: no remote copies, remote signals or barrier semaphores. Data moves between devices by JAX's collectives and lax.ppermute only.
A program may use at most 128 MiB of HBM per device.

```python
import math
import jax
import jax.numpy as jnp
from jax import lax

NY = 1024
NZ = 1024
XP = 1
NBP = 8
NBQ = 16
NB_W = 8
NT = 32
NW = 32


def level_of(key, wavenum, count, length):
    width = (length // 2 + 1) // count
    jitter = jax.random.randint(key, (count - 1,), 0, width)
    edges = (jnp.arange(1, count, dtype=jnp.int32) * width + jitter).astype(jnp.int32)
    return jnp.sum((wavenum[:, None] >= edges[None, :]).astype(jnp.int32), axis=1)


def draw_mode_bin(key, part):
    wave_y = jnp.arange(NY, dtype=jnp.int32)
    wave_z = jnp.arange(NZ, dtype=jnp.int32)
    perp_level = level_of(jax.random.fold_in(key, 11), jnp.minimum(wave_y, NY - wave_y), NBQ, NY)
    para_level = level_of(jax.random.fold_in(key, 23), jnp.minimum(wave_z, NZ - wave_z), NBP, NZ)
    return (para_level[None, :] * NBQ + perp_level[:, None]).astype(jnp.int32)


def draw_omega_edges(key, part):
    picks = jax.random.permutation(key, NW - 1)[:NB_W - 1] + 1
    inner = jnp.sort(picks).astype(jnp.int32)
    first = jnp.zeros((1,), jnp.int32)
    final = jnp.full((1,), NW, jnp.int32)
    return jnp.concatenate([first, inner, final])


def block_scale(rng, shape, pieces, least, high):
    gain = 1.0
    for dim, blocks in pieces:
        steps = jax.random.uniform(jax.random.fold_in(jax.random.fold_in(rng, 6), dim), (blocks,), jnp.float32, least / len(pieces), high / len(pieces))
        gain = gain * jnp.repeat(jnp.exp(steps), shape[dim] // blocks).reshape((-1,) + (1,) * (len(shape) - 1 - dim))
    return gain


def gaussian(own_key, extent, scale, most, cuts=(), kind=jnp.bfloat16):
    values = scale * jax.random.normal(own_key, extent, jnp.float32)
    if cuts:
        values = values * block_scale(own_key, extent, cuts, -0.22, 0.18)
    return jnp.clip(values, -most, most).astype(kind)


def setup_inputs(seed: int = 0) -> dict:
    key_of = jax.random.split(jax.random.key(seed), 5)
    magnetic = gaussian(key_of[0], (NT, 3, XP + 2, NY, NZ), 1.0, 6.0, ((0, 32), (3, 8)))
    velocity = gaussian(key_of[1], (NT, 3, XP, NY, NZ), 1.0, 6.0, ((0, 32), (3, 8)))
    mode_bin = draw_mode_bin(jax.random.fold_in(key_of[4], 71), 0)
    omega_edges = draw_omega_edges(jax.random.fold_in(key_of[4], 71), 0)
    return dict(magnetic=magnetic, velocity=velocity, mode_bin=mode_bin, omega_edges=omega_edges)


hall_coef = 1.0
highest = lax.Precision.HIGHEST


def window_taper_for(sample_moments, every_time_sample):
    return 0.5 - 0.5 * jnp.cos(2.0 * math.pi * (sample_moments.astype(jnp.float32) + 0.5) / every_time_sample)


def temporal_coefficients(angular_frequency, sample_moments, every_time_sample):
    phase_angles = jnp.mod(angular_frequency[:, None] * sample_moments[None, :], every_time_sample).astype(jnp.float32)
    angles = 2.0 * math.pi * phase_angles / every_time_sample
    taper_weight = window_taper_for(sample_moments, every_time_sample)[None, :]
    return (taper_weight * jnp.cos(angles)).astype(jnp.bfloat16), (-taper_weight * jnp.sin(angles)).astype(jnp.bfloat16)


def dft_tables(length):
    series = jnp.arange(length, dtype=jnp.int32)
    phase_angles = jnp.mod(series[:, None] * series[None, :], length).astype(jnp.float32)
    angles = 2.0 * math.pi * phase_angles / length
    return jnp.cos(angles).astype(jnp.bfloat16), jnp.sin(angles).astype(jnp.bfloat16)


def z_slope(values):
    return (jnp.roll(values, -1, axis=-1) - jnp.roll(values, 1, axis=-1)) * 0.5


def electric_of(magnetic, velocity, slope_magz, slope_magx):
    inner = magnetic[:, :, 1:-1].astype(jnp.float32)
    x_slope = (magnetic[:, :, 2:].astype(jnp.float32) - magnetic[:, :, :-2].astype(jnp.float32)) * 0.5
    mag_x, mag_y, mag_z = inner[:, 0], inner[:, 1], inner[:, 2]
    cur_x = slope_magz - z_slope(mag_y)
    cur_y = z_slope(mag_x) - x_slope[:, 2]
    cur_z = x_slope[:, 1] - slope_magx
    flow = velocity.astype(jnp.float32)
    vel_x, vel_y, vel_z = flow[:, 0], flow[:, 1], flow[:, 2]
    elec_x = -(vel_y * mag_z - vel_z * mag_y) + hall_coef * (cur_y * mag_z - cur_z * mag_y)
    elec_y = -(vel_z * mag_x - vel_x * mag_z) + hall_coef * (cur_z * mag_x - cur_x * mag_z)
    elec_z = -(vel_x * mag_y - vel_y * mag_x) + hall_coef * (cur_x * mag_y - cur_y * mag_x)
    return jnp.stack([elec_x, elec_y, elec_z], axis=1)


def reference(magnetic, velocity, mode_bin, omega_edges):
    plane_z = magnetic[:, 2, 1:-1].astype(jnp.float32)
    plane_x = magnetic[:, 0, 1:-1].astype(jnp.float32)
    slope_magz = (jnp.roll(plane_z, -1, axis=2) - jnp.roll(plane_z, 1, axis=2)) * 0.5
    slope_magx = (jnp.roll(plane_x, -1, axis=2) - jnp.roll(plane_x, 1, axis=2)) * 0.5
    electric = electric_of(magnetic, velocity, slope_magz, slope_magx).astype(jnp.bfloat16)
    moments = jnp.arange(NT, dtype=jnp.int32)
    coef_re, coef_im = temporal_coefficients(moments - NT // 2, moments, NT)
    samples = electric.astype(jnp.float32)
    timed_re = jnp.einsum("wt,tcxyz->wcxyz", coef_re.astype(jnp.float32), samples, precision=highest).astype(jnp.bfloat16)
    timed_im = jnp.einsum("wt,tcxyz->wcxyz", coef_im.astype(jnp.float32), samples, precision=highest).astype(jnp.bfloat16)
    zcos_tab, zsin_tab = dft_tables(NZ)
    zcos_f = zcos_tab.astype(jnp.float32)
    zsin_f = zsin_tab.astype(jnp.float32)
    part_re = timed_re.astype(jnp.float32)
    part_im = timed_im.astype(jnp.float32)
    zturn_re = (jnp.einsum("wcxyz,zk->wcxyk", part_re, zcos_f, precision=highest) + jnp.einsum("wcxyz,zk->wcxyk", part_im, zsin_f, precision=highest)).astype(jnp.bfloat16)
    zturn_im = (jnp.einsum("wcxyz,zk->wcxyk", part_im, zcos_f, precision=highest) - jnp.einsum("wcxyz,zk->wcxyk", part_re, zsin_f, precision=highest)).astype(jnp.bfloat16)
    ycos_tab, ysin_tab = dft_tables(NY)
    ycos_f = ycos_tab.astype(jnp.float32)
    ysin_f = ysin_tab.astype(jnp.float32)
    mid_re = zturn_re.astype(jnp.float32)
    mid_im = zturn_im.astype(jnp.float32)
    wave_re = jnp.einsum("wcxyk,yq->wcxqk", mid_re, ycos_f, precision=highest) + jnp.einsum("wcxyk,yq->wcxqk", mid_im, ysin_f, precision=highest)
    wave_im = jnp.einsum("wcxyk,yq->wcxqk", mid_im, ycos_f, precision=highest) - jnp.einsum("wcxyk,yq->wcxqk", mid_re, ysin_f, precision=highest)
    power = jnp.sum(wave_re * wave_re + wave_im * wave_im, axis=(1, 2)) / (NT * NY * NZ)
    by_mode = jax.ops.segment_sum(power.reshape(NW, NY * NZ).T, mode_bin.reshape(-1), num_segments=NBP * NBQ)
    omega = jnp.arange(NW, dtype=jnp.int32)
    member = ((omega[None, :] >= omega_edges[:-1, None]) & (omega[None, :] < omega_edges[1:, None])).astype(jnp.float32)
    binned = jnp.dot(member, by_mode.T, precision=highest)
    spectrum = jnp.log(binned * (NB_W * NBP * NBQ) / (NW * NY * NZ) + 1e-6)
    return power, spectrum
```

```python
import math

import jax
import jax.numpy as jnp
import numpy as np
from jax import lax
from jax.experimental import pallas as pl
from jax.experimental.pallas import tpu as pltpu
from jax.sharding import PartitionSpec as P

NBP = 8
NBQ = 16
NB_W = 8
BINS = NBP * NBQ
N = 1024
NT = 32
SLAB = 128
HALF = NT // 2
f32 = jnp.float32
bf16 = jnp.bfloat16
VMEM = pl.BlockSpec(memory_space=pltpu.VMEM)


def electric_kernel(mag_ref, vel_ref, low_ref, high_ref, out_ref, bx_ref, bz_ref):
    bx_ref[0:8, :] = jnp.broadcast_to(low_ref[0:1, :].astype(f32), (8, N))
    bz_ref[0:8, :] = jnp.broadcast_to(low_ref[1:2, :].astype(f32), (8, N))
    bx_ref[SLAB + 8 : SLAB + 16, :] = jnp.broadcast_to(high_ref[0:1, :].astype(f32), (8, N))
    bz_ref[SLAB + 8 : SLAB + 16, :] = jnp.broadcast_to(high_ref[1:2, :].astype(f32), (8, N))

    def widen(group, carry):
        rows = pl.ds(pl.multiple_of(group * 8, 8), 8)
        inside = pl.ds(pl.multiple_of(group * 8 + 8, 8), 8)
        bx_ref[inside, :] = mag_ref[0, 0, 1, rows, :].astype(f32)
        bz_ref[inside, :] = mag_ref[0, 2, 1, rows, :].astype(f32)
        return carry

    lax.fori_loop(0, SLAB // 8, widen, 0)
    row = lax.broadcasted_iota(jnp.int32, (8, N), 0)
    half_row = lax.broadcasted_iota(jnp.int32, (8, 128), 0)

    def y_slope(ref, group):
        before = ref[pl.ds(pl.multiple_of(group * 8, 8), 8), :]
        here = ref[pl.ds(pl.multiple_of(group * 8 + 8, 8), 8), :]
        after = ref[pl.ds(pl.multiple_of(group * 8 + 16, 8), 8), :]
        up = jnp.where(row == 7, pltpu.roll(after, 7, 0), pltpu.roll(here, 7, 0))
        down = jnp.where(row == 0, pltpu.roll(before, 1, 0), pltpu.roll(here, 1, 0))
        return here, (up - down) * 0.5

    def z_slope(v):
        return (pltpu.roll(v, N - 1, 1) - pltpu.roll(v, 1, 1)) * 0.5

    def step(group, carry):
        rows = pl.ds(pl.multiple_of(group * 8, 8), 8)

        def x_slope(c):
            return (mag_ref[0, c, 2, rows, :].astype(f32) - mag_ref[0, c, 0, rows, :].astype(f32)) * 0.5

        mag_x, slope_x = y_slope(bx_ref, group)
        mag_z, slope_z = y_slope(bz_ref, group)
        mag_y = mag_ref[0, 1, 1, rows, :].astype(f32)
        cur_x = slope_z - z_slope(mag_y)
        cur_y = z_slope(mag_x) - x_slope(2)
        cur_z = x_slope(1) - slope_x
        vel_x = vel_ref[0, 0, 0, rows, :].astype(f32)
        vel_y = vel_ref[0, 1, 0, rows, :].astype(f32)
        vel_z = vel_ref[0, 2, 0, rows, :].astype(f32)
        field = (
            -(vel_y * mag_z - vel_z * mag_y) + (cur_y * mag_z - cur_z * mag_y),
            -(vel_z * mag_x - vel_x * mag_z) + (cur_z * mag_x - cur_x * mag_z),
            -(vel_x * mag_y - vel_y * mag_x) + (cur_x * mag_y - cur_y * mag_x),
        )
        for c in range(3):
            for a in range(4):
                first = field[c][:, 128 * a : 128 * a + 128]
                second = field[c][:, 128 * a + 512 : 128 * a + 640]
                even = jnp.where(half_row < 4, first, pltpu.roll(second, 4, 0))
                odd = jnp.where(half_row < 4, pltpu.roll(first, 4, 0), second)
                out_ref[2 * group, 4 * c + a] = even.astype(bf16)
                out_ref[2 * group + 1, 4 * c + a] = odd.astype(bf16)
        return carry

    lax.fori_loop(0, SLAB // 8, step, 0)


def electric(magnetic, velocity, low, high):
    return pl.pallas_call(
        electric_kernel,
        out_shape=jax.ShapeDtypeStruct((NT, 12, 8, 128), bf16),
        in_specs=[VMEM] * 4,
        out_specs=VMEM,
        scratch_shapes=[pltpu.VMEM((SLAB + 16, N), f32)] * 2,
        compiler_params=pltpu.CompilerParams(vmem_limit_bytes=24 << 20),
        cost_estimate=pl.CostEstimate(flops=8000000, bytes_accessed=4000000, transcendentals=0),
        name="electric",
    )(magnetic, velocity, low, high)


def small_tables(wave, quarter):
    def pair(rows, scale, back):
        phase = (np.arange(rows)[:, None] * scale * wave[None, :] - back[None, :]) % N
        angle = 2.0 * np.pi * phase / N
        return np.cos(angle).astype(np.float32), np.sin(angle).astype(np.float32)

    none = np.zeros_like(wave)
    return pair(8, 1, 256 * quarter) + pair(8, 8, none) + pair(16, 64, none)


def table_kernel(rc_ref, rs_ref, ic_ref, is_ref, mc_ref, ms_ref, *out_refs):
    m = pl.program_id(0)
    mc = mc_ref[pl.ds(m, 1), :]
    ms = ms_ref[pl.ds(m, 1), :]
    for lanes in range(0, rc_ref.shape[1], 512):
        cut = slice(lanes, lanes + 512)
        mid_c = ic_ref[:, cut] * mc[:, cut] - is_ref[:, cut] * ms[:, cut]
        mid_s = is_ref[:, cut] * mc[:, cut] + ic_ref[:, cut] * ms[:, cut]
        rc = rc_ref[:, cut]
        rs = rs_ref[:, cut]
        for i in range(0, 8, 2):
            cos_rows = []
            sin_rows = []
            for k in (i, i + 1):
                c = jnp.broadcast_to(mid_c[k : k + 1, :], rc.shape)
                s = jnp.broadcast_to(mid_s[k : k + 1, :], rc.shape)
                cos_rows.append(rc * c - rs * s)
                if len(out_refs) == 2:
                    sin_rows.append(-(rs * c) - rc * s)
            out_refs[0][8 * i : 8 * i + 16, cut] = jnp.concatenate(cos_rows, axis=0).astype(bf16)
            if len(out_refs) == 2:
                out_refs[1][8 * i : 8 * i + 16, cut] = jnp.concatenate(sin_rows, axis=0).astype(bf16)


def tables(small, count, name):
    width = small[0].shape[1]
    whole = lambda a: pl.BlockSpec(a.shape, lambda m: (0, 0))
    return pl.pallas_call(
        table_kernel,
        grid=(16,),
        out_shape=[jax.ShapeDtypeStruct((N, width), bf16)] * count,
        in_specs=[whole(a) for a in small],
        out_specs=[pl.BlockSpec((64, width), lambda m: (m, 0))] * count,
        cost_estimate=pl.CostEstimate(
            flops=12000000, bytes_accessed=count * N * width * 2, transcendentals=0
        ),
        name=name,
    )(*small)


def time_matrix():
    t = np.arange(NT)
    taper = 0.5 - 0.5 * np.cos(2.0 * np.pi * (t + 0.5) / NT)
    table = np.zeros((HALF, 2, NT))
    for f in range(HALF):
        angle = 2.0 * np.pi * ((f * t) % NT) / NT
        table[f, 0] = taper * np.cos(angle)
        table[f, 1] = -taper * np.sin(angle)
    table[0, 1] = taper * np.cos(2.0 * np.pi * ((HALF * t) % NT) / NT)
    spread = np.einsum("fpt,bd,ye->bfpytde", table, np.eye(2), np.eye(4))
    return spread.reshape(256, 256).astype(np.float32).astype(jnp.bfloat16)


def turn_kernel(field_ref, time_ref, table_ref, out_ref, left_ref):
    for c in range(3):
        cells = jnp.concatenate(
            [field_ref[:, 4 * c + a].reshape(NT * 8, 128) for a in range(4)], axis=1
        )
        timed = jnp.dot(time_ref[...], cells, preferred_element_type=f32).astype(bf16)
        left_ref[128 * c : 128 * c + 128, 0:512] = timed[0:128]
        left_ref[128 * c : 128 * c + 128, 512:1024] = timed[128:256]
    left = left_ref[...]
    row = lax.broadcasted_iota(jnp.int32, (8, 128), 0)
    for g in range(8):
        by_cos = jnp.dot(
            left, table_ref[:, 128 * g : 128 * g + 128], preferred_element_type=f32
        ).reshape(3, HALF, 8, 128)
        by_sin = jnp.dot(
            left, table_ref[:, N + 128 * g : N + 128 * g + 128], preferred_element_type=f32
        ).reshape(3, HALF, 8, 128)
        for c in range(3):
            for f in range(HALF):
                pc, ps = by_cos[c, f], by_sin[c, f]
                swapped = pltpu.roll(ps, 4, 0)
                if f == 0:
                    plus = jnp.where(row < 4, pc, -swapped)
                    minus = jnp.where(row < 4, pltpu.roll(pc, 4, 0), -ps)
                    low = 0
                else:
                    plus = jnp.where(row < 4, pc + swapped, pc - swapped)
                    minus = jnp.where(row < 4, pc - swapped, -pc - swapped)
                    low = HALF - f
                out_ref[(HALF + f) * 8 + g, c] = plus.astype(bf16)
                out_ref[low * 8 + g, c] = minus.astype(bf16)


def turn(field, time_table, table):
    return pl.pallas_call(
        turn_kernel,
        out_shape=jax.ShapeDtypeStruct((NT * 8, 3, 8, 128), bf16),
        in_specs=[VMEM] * 3,
        out_specs=VMEM,
        scratch_shapes=[pltpu.VMEM((384, N), bf16)],
        compiler_params=pltpu.CompilerParams(vmem_limit_bytes=32 << 20),
        cost_estimate=pl.CostEstimate(
            flops=2 * 384 * N * 2 * N, bytes_accessed=8000000, transcendentals=0
        ),
        name="turn",
    )(field, time_table, table)


ROWS = 256


def split_dot(exact, value, dims):
    high = value.astype(bf16)
    rest = (value - high.astype(f32)).astype(bf16)
    dot = lambda v: lax.dot_general(exact, v, dims, preferred_element_type=f32)
    return dot(high) + dot(rest)


def power_kernel(cells_ref, re_ref, im_ref, bins_ref, head_ref, power_ref, binned_ref, right_ref, sum_ref):
    step = pl.program_id(0)

    @pl.when(step == 0)
    def _():
        for c in range(3):
            right_ref[:, 128 * c : 128 * c + 128] = cells_ref[:, c].reshape(2 * N, 128)
        sum_ref[...] = jnp.zeros_like(sum_ref)

    wave_re = jnp.dot(re_ref[...], right_ref[...], preferred_element_type=f32)
    wave_im = jnp.dot(im_ref[...], right_ref[...], preferred_element_type=f32)
    square = wave_re * wave_re + wave_im * wave_im
    power = (square[:, 0:128] + square[:, 128:256] + square[:, 256:384]) * (1.0 / (NT * N * N))
    power_ref[0] = power
    lane = lax.broadcasted_iota(jnp.int32, (ROWS, BINS), 1)
    same_q = ((bins_ref[...] & (NBQ - 1)) == (lane & (NBQ - 1))).astype(f32).astype(bf16)
    sum_ref[...] += split_dot(same_q, power, (((0,), (0,)), ((), ())))

    @pl.when(step == N // ROWS - 1)
    def _():
        bin_row = lax.broadcasted_iota(jnp.int32, (BINS, SLAB), 0)
        by_bin = jnp.where(head_ref[...] // NBQ == bin_row // NBQ, sum_ref[...], 0.0)
        ones = jnp.ones((8, SLAB), bf16)
        binned_ref[...] = split_dot(ones, by_bin, (((1,), (1,)), ((), ())))[0:1]


def power_of(cells, re_table, im_table, mode_bin):
    return pl.pallas_call(
        power_kernel,
        grid=(N // ROWS,),
        out_shape=[
            jax.ShapeDtypeStruct((1, N, SLAB), f32),
            jax.ShapeDtypeStruct((1, BINS), f32),
        ],
        in_specs=[
            pl.BlockSpec((NT * 8, 3, 8, 128), lambda i: (0, 0, 0, 0)),
            pl.BlockSpec((ROWS, 2 * N), lambda i: (i, 0)),
            pl.BlockSpec((ROWS, 2 * N), lambda i: (i, 0)),
            pl.BlockSpec((ROWS, SLAB), lambda i: (i, 0)),
            pl.BlockSpec((BINS, SLAB), lambda i: (0, 0)),
        ],
        out_specs=[
            pl.BlockSpec((1, ROWS, SLAB), lambda i: (0, i, 0)),
            pl.BlockSpec((1, BINS), lambda i: (0, 0)),
        ],
        scratch_shapes=[pltpu.VMEM((2 * N, 384), bf16), pltpu.VMEM((BINS, SLAB), f32)],
        compiler_params=pltpu.CompilerParams(vmem_limit_bytes=32 << 20),
        cost_estimate=pl.CostEstimate(
            flops=2 * 2 * N * 2 * N * 384, bytes_accessed=12000000, transcendentals=0
        ),
        name="power",
    )(cells, re_table, im_table, mode_bin, mode_bin)


Z_SMALL = small_tables(np.arange(2 * N) % N, np.arange(2 * N) // N)


def y_columns():
    column = np.arange(2 * N)
    source = column // 8
    plane = SLAB * (source % 8) + 4 * (source // 8) + column % 4
    return plane, column // 4 % 2


Y_SMALL = small_tables(*y_columns())
TIME_TABLE = time_matrix()


def body(magnetic, velocity, mode_bin, omega_edges):
    ring = lax.axis_size("gy")
    first = jnp.stack([magnetic[0, 0, 1, 0], magnetic[0, 2, 1, 0]])
    last = jnp.stack([magnetic[0, 0, 1, SLAB - 1], magnetic[0, 2, 1, SLAB - 1]])
    low = lax.ppermute(last, "gy", [(i, (i + 1) % ring) for i in range(ring)])
    high = lax.ppermute(first, "gy", [((i + 1) % ring, i) for i in range(ring)])
    field = electric(magnetic, velocity, low, high)
    field = lax.all_to_all(field.reshape(NT, 96, 128), "tm", 0, 0, tiled=True)
    (z_table,) = tables([jnp.asarray(a) for a in Z_SMALL], 1, "z_table")
    turned = turn(field.reshape(NT, 12, 8, 128), jnp.asarray(TIME_TABLE), z_table)
    cells = lax.all_to_all(turned.reshape(NT * 8, 24, 128), ("tm", "gy"), 0, 0, tiled=True)
    re_table, im_table = tables([jnp.asarray(a) for a in Y_SMALL], 2, "y_table")
    power, by_mode = power_of(cells.reshape(NT * 8, 3, 8, 128), re_table, im_table, mode_bin)
    spread = jnp.broadcast_to(by_mode[None], (NT * 8, 1, BINS))
    every = lax.all_to_all(spread, ("tm", "gy"), 0, 0, tiled=True).reshape(NT, 8, BINS)
    omega = jnp.arange(NT, dtype=jnp.int32)
    member = (omega[None, :] >= omega_edges[:-1, None]) & (omega[None, :] < omega_edges[1:, None])
    binned = jnp.sum(jnp.where(member[:, :, None, None], every[None], 0.0), axis=(1, 2))
    spectrum = jnp.log(binned * (NB_W * BINS) / (NT * N * N) + 1e-06)
    return power, spectrum


def solution(mesh):
    return jax.shard_map(
        body,
        mesh=mesh,
        in_specs=(
            P("tm", None, None, "gy", None),
            P("tm", None, None, "gy", None),
            P(None, "gy"),
            P(),
        ),
        out_specs=(P("tm", None, "gy"), P()),
        check_vma=False,
    )
```
